256 devices in a mesh: row: 16 (over z, core), col: 16 (over x, y).
Axes of the slice: x: 4, y: 4, z: 8, core: 2. Of those that a mesh axis runs over, the one named last changes fastest.
Arguments:
- work: float32 [8192, 8192], P('row', 'col'), may hold values from -6 to 6
- a_tiles: bfloat16 [16, 16, 512, 512], P('row', None, 'col'), may hold values from -0.078125 to 0.078125
- b_tiles: bfloat16 [16, 16, 512, 512], P(None, 'col', 'row'), may hold values from -0.078125 to 0.078125
- u_powers: float32 [16, 3, 512, 512], P('row', None, 'col'), may hold values from -1 to 1, as said below
- v_powers: float32 [16, 3, 512, 512], P('col', None, 'row'), may hold values from -1 to 1, as said below
- shift: float32 [1], replicated, may hold values from 0.5 to 2
Outputs:
- progress: float32 [8192, 8192], P('row', 'col')
The draws below stay inside these ranges and needn't reach their ends.
Inputs may be any that keep to these rules, and one draw needn't show every extreme that they name: u_powers[i] holds U, U^2 and U^4 for a lower triangular U whose diagonal entries have magnitudes 0.3 to 0.9. v_powers[j] holds V, V^2 and V^4 for an upper triangular V whose diagonal entries have magnitudes 0.3 to 0.9.
All inputs are finite; a program needn't handle non-finite values.
Results may differ from the reference program's by a relative error of at most 0.0023.
Values may be sent and summed in bfloat16 or wider, within the bound.
No kernel may reach another device: no remote copies, remote signals or barrier semaphores. Data moves between devices by JAX's collectives and lax.ppermute only.
A program may use at most 128 MiB of HBM per device.

```python
import math
import jax
import jax.numpy as jnp
import numpy as np
from jax import lax

T_SIZE = 512
FRONTS = 3
TROWS = 16
TCOLS = 16
FIRST = 13


def triangle_stack(key, count, lower):
    first_key, second_key, third_key = jax.random.split(key, 3)
    magnitude = jax.random.uniform(first_key, (count, T_SIZE), jnp.float32, 0.3, 0.85)
    signs = jnp.where(jax.random.bernoulli(second_key, 0.5, (count, T_SIZE)), 1.0, -1.0)
    spread = jax.random.normal(third_key, (count, T_SIZE, T_SIZE), jnp.float32) * (0.3 / jnp.sqrt(1.0 * T_SIZE))
    spread = jnp.clip(spread, -6.0 * 0.3 / jnp.sqrt(1.0 * T_SIZE), 6.0 * 0.3 / jnp.sqrt(1.0 * T_SIZE))
    identity = jnp.eye(T_SIZE, dtype=jnp.float32)
    if lower:
        strict = jnp.tril(spread, -1)
    else:
        strict = jnp.triu(spread, 1)
    base = strict + (magnitude * signs)[:, :, None] * identity[None]
    square = jnp.einsum('nab,nbc->nac', base, base, precision=lax.Precision.HIGHEST)
    fourth = jnp.einsum('nab,nbc->nac', square, square, precision=lax.Precision.HIGHEST)
    return jnp.stack([base, square, fourth], axis=1)


def draw_u_powers(key, part):
    return triangle_stack(jax.random.fold_in(key, 11), TROWS, True)


def draw_v_powers(key, part):
    return triangle_stack(jax.random.fold_in(key, 23), TCOLS, False)


def block_scale(own_key, extent, cuts, low, largest):
    def one(axis_at, parts):
        heights = jax.random.uniform(jax.random.fold_in(jax.random.fold_in(own_key, 6), axis_at), (parts,), jnp.float32, low / len(cuts), largest / len(cuts))
        return jnp.repeat(jnp.exp(heights), extent[axis_at] // parts).reshape((-1,) + (1,) * (len(extent) - axis_at - 1))

    gain = one(*cuts[0])
    for cut in cuts[1:]:
        gain = gain * one(*cut)
    return gain


def scatter_about(rng, shape, scale, most, cuts=(), kind=jnp.bfloat16):
    loudness = block_scale(rng, shape, cuts, -0.22, 0.18) if cuts else 1.0
    values = jax.random.normal(rng, shape, jnp.float32) * scale * loudness
    return jnp.minimum(jnp.maximum(values, -most), most).astype(kind)


def setup_inputs(seed: int = 0) -> dict:
    streams_of = jax.random.split(jax.random.key(seed), 7)
    return {
        "work": scatter_about(streams_of[0], (TROWS * T_SIZE, TCOLS * T_SIZE), 1.0, 6.0, ((0, 16), (1, 16)), jnp.float32),
        "a_tiles": scatter_about(streams_of[1], (TROWS, TROWS, T_SIZE, T_SIZE), (4 * T_SIZE * FRONTS) ** -0.5, 0.078125, ((0, 16), (2, 16))),
        "b_tiles": scatter_about(streams_of[2], (TCOLS, TCOLS, T_SIZE, T_SIZE), (4 * T_SIZE * FRONTS) ** -0.5, 0.078125, ((1, 16), (2, 16))),
        "u_powers": draw_u_powers(jax.random.fold_in(streams_of[6], 71), 0),
        "v_powers": draw_v_powers(jax.random.fold_in(streams_of[6], 71), 0),
        "shift": jnp.clip(jnp.exp(jax.random.uniform(streams_of[5], (1,), jnp.float32, math.log(0.5), math.log(2.0))), 0.5, 2.0),
    }


finest = lax.Precision.HIGHEST


def solve_tiles(source, u_stack, v_stack, shift_value):
    identity = jnp.eye(T_SIZE, dtype=jnp.float32)
    left_factor = identity - u_stack[:, 0]
    right_factor = identity - v_stack[:, 0]
    current = jnp.einsum("nab,nbc->nac", left_factor, source, precision=finest)
    current = jnp.einsum("nab,nbc->nac", current, right_factor, precision=finest) / (2.0 * shift_value)
    for power in range(3):
        moved = jnp.einsum("nab,nbc->nac", u_stack[:, power], current, precision=finest)
        current = current + jnp.einsum("nab,nbc->nac", moved, v_stack[:, power], precision=finest)
    return current


def rounded(values):
    narrow = lax.optimization_barrier(values.astype(jnp.bfloat16))
    return narrow.astype(jnp.float32)


def reference(work, a_tiles, b_tiles, u_powers, v_powers, shift):
    state = work.reshape(TROWS, T_SIZE, TCOLS, T_SIZE).transpose(0, 2, 1, 3)
    a_full = a_tiles.astype(jnp.float32)
    b_full = b_tiles.astype(jnp.float32)
    front_map = np.arange(TROWS)[:, None] + np.arange(TCOLS)[None, :]
    for number in range(FRONTS):
        front = FIRST + number
        row_list = [place for place in range(TROWS) if 0 <= front - place < TCOLS]
        row_index = np.array(row_list, dtype=np.int32)
        col_index = (front - row_index).astype(np.int32)
        solved = solve_tiles(state[row_index, col_index], u_powers[row_index], v_powers[col_index], shift[0])
        state = state.at[row_index, col_index].set(solved)
        down_rows = front - np.arange(TCOLS)
        valid_down = (down_rows >= 0) & (down_rows < TROWS)
        down_rows = np.clip(down_rows, 0, TROWS - 1).astype(np.int32)
        across_cols = front - np.arange(TROWS)
        valid_across = (across_cols >= 0) & (across_cols < TCOLS)
        across_cols = np.clip(across_cols, 0, TCOLS - 1).astype(np.int32)
        down_tiles = rounded(state[down_rows, np.arange(TCOLS)])
        across_tiles = rounded(state[np.arange(TROWS), across_cols])
        term_a = jnp.einsum("ijab,jbc->ijac", a_full[:, down_rows], down_tiles, precision=finest)
        term_b = jnp.einsum("iab,ijbc->ijac", across_tiles, b_full[across_cols], precision=finest)
        term = jnp.where(valid_down[None, :, None, None], term_a, 0.0) + jnp.where(valid_across[:, None, None, None], term_b, 0.0)
        state = jnp.where((front_map > front)[:, :, None, None], state - term, state)
    return state.transpose(0, 2, 1, 3).reshape(TROWS * T_SIZE, TCOLS * T_SIZE)
```

```python
import jax
import jax.numpy as jnp
import numpy as np
from jax import lax
from jax.sharding import PartitionSpec as P

FRONTS = 3
CORES = 2

half_type = jnp.bfloat16


def split(values):
    high = lax.reduce_precision(values, 8, 7)
    return high.astype(half_type), (values - high).astype(half_type)


def product(left_side, right_side):
    return jnp.dot(
        left_side, right_side, preferred_element_type=jnp.float32, precision=lax.Precision.HIGH
    )


def narrow(left_side, right_side):
    return jnp.dot(left_side, right_side, preferred_element_type=jnp.float32)


def exchange(array, axis):
    return lax.all_to_all(array, axis, split_axis=0, concat_axis=0, tiled=True)


class Grid:
    def __init__(self, rows, cols):
        self.rows, self.cols, self.deep = rows, cols, rows // CORES

    def place(self, i, j):
        return i * self.cols + j

    def front(self, number):
        return [(i, number - i) for i in range(self.rows) if 0 <= number - i < self.cols]

    def moved(self, number, down, right):
        return [
            (self.place(i, j), self.place(i + down, j + right))
            for i, j in self.front(number)
            if i + down < self.rows and j + right < self.cols
        ]

    def every(self, target_of, wanted):
        pairs = []
        for i in range(self.rows):
            for j in range(self.cols):
                k, l = target_of(i, j)
                if wanted(k, l):
                    pairs.append((self.place(i, j), self.place(k, l)))
        return pairs

    def deeper(self, step, wanted):
        return self.every(lambda i, j: ((i + CORES * step) % self.rows, j), wanted)

    def partner(self):
        return self.every(lambda i, j: (i ^ 1, j), lambda i, j: True)

    def tree(self, number):
        steps = [[] for _ in range(self.deep.bit_length() - 1)]
        for i, j in self.front(number):
            root = i // CORES
            for core in range(CORES):
                sign = 1 if core == 0 else -1

                def reach(at, level):
                    size = self.deep >> (level + 1)
                    if size == 0:
                        return at > root
                    there = (at + sign * size) % self.deep
                    used = reach(at, level + 1)
                    if reach(there, level + 1):
                        used = True
                    return used

                def walk(at, level):
                    size = self.deep >> (level + 1)
                    if size == 0:
                        return
                    there = (at + sign * size) % self.deep
                    if reach(there, level + 1):
                        steps[level].append(
                            (self.place(CORES * at + core, j), self.place(CORES * there + core, j))
                        )
                        walk(there, level + 1)
                    walk(at, level + 1)

                walk(root, 0)
        return steps


def send(array, pairs):
    return lax.ppermute(array, ("row", "col"), pairs)


def per_device(work, a_tiles, b_tiles, u_powers, v_powers, shift):
    rows = lax.axis_size("row")
    cols = lax.axis_size("col")
    grid = Grid(rows, cols)
    deep = grid.deep
    i = lax.axis_index("row")
    j = lax.axis_index("col")
    z, core = i // CORES, i % CORES
    diagonal = i + j
    first = max(0, (rows + cols) // 2 - FRONTS)
    last = first + FRONTS - 1
    width = work.shape[0]
    strip = width // cols
    half = width // 2
    even = core == 0

    def strips(tile):
        return tile.reshape(cols, tile.shape[0] // cols, width)

    def whole(parts):
        return parts.reshape(width, width)

    a_strips = [
        a_tiles[0, ((first + n - np.arange(cols)) % cols).astype(np.int32)] for n in range(FRONTS)
    ]
    u_high, u_low = split(u_powers[0, 0])
    opening = exchange(
        jnp.concatenate(
            [
                jnp.broadcast_to(u_high, (cols, strip, width)),
                jnp.broadcast_to(u_low, (cols, strip, width)),
                a_strips[0],
            ],
            axis=1,
        ),
        "col",
    )

    near = {n: set() for n in range(cols)}
    for n in range(FRONTS):
        for r, c in grid.front(first + n):
            near[c].add(r // CORES)
    v_high, v_low = split(v_powers[0, 0])
    v_mine = jnp.concatenate([v_high, v_low], axis=0)
    v_all = [v_mine]
    for step in range(1, deep):
        v_all.append(send(v_mine, grid.deeper(step, lambda k, l: k // CORES in near[l])))
    arrived = (z - jnp.arange(deep)) % deep
    v_here = jnp.stack(v_all)[arrived]
    v_there = send(v_here, grid.partner())
    v_full = jnp.stack(
        [jnp.where(even, v_here, v_there), jnp.where(even, v_there, v_here)], axis=1
    ).reshape(deep, CORES, 2, strip, width)

    b_strips = b_tiles[((first - np.arange(rows)) % rows).astype(np.int32), 0].reshape(
        deep, CORES, strip, width
    )
    b_mine = jnp.where(even, b_strips[:, 0], b_strips[:, 1])
    b_other = send(jnp.where(even, b_strips[:, 1], b_strips[:, 0]), grid.partner())
    b_pairs = jnp.concatenate(
        [jnp.where(even, b_mine, b_other), jnp.where(even, b_other, b_mine)], axis=1
    )[(z + jnp.arange(deep)) % deep]
    b_all = [b_pairs[0]]
    for step in range(1, deep):
        b_all.append(
            send(b_pairs[step], grid.deeper(step, lambda k, l: k + l > first or k > first))
        )
    b_full = [whole(jnp.stack(b_all)[arrived])]
    for n in range(1, FRONTS):
        b_full.append(
            send(
                b_full[0],
                grid.every(
                    lambda k, l: ((k + n) % rows, l),
                    lambda k, l: k + l > first + n and k <= first + n,
                ),
            )
        )

    u_base = whole(opening[:, :strip]).astype(jnp.float32) + whole(
        opening[:, strip : 2 * strip]
    ).astype(jnp.float32)
    a_full = [whole(opening[:, 2 * strip :])]
    v_base = whole(v_full[:, :, 0]).astype(jnp.float32) + whole(v_full[:, :, 1]).astype(jnp.float32)
    identity = jnp.eye(width, dtype=jnp.float32)
    u_square = product(u_base, u_base)
    v_square = product(v_base, v_base)
    u_list = [u_base, u_square, product(u_square, u_square)]
    v_list = [v_base, v_square, product(v_square, v_square)]
    left_factor = identity - u_base
    right_factor = (identity - v_base) / (2.0 * shift[0])

    def solve(source):
        current = product(product(left_factor, source), right_factor)
        for power in range(3):
            current = current + product(product(u_list[power], current), v_list[power])
        return current

    def spread_deep(sent, number):
        halves = sent.reshape(2, half, width)
        mine = jnp.where(even, halves[0], halves[1])
        given = send(jnp.where(even, halves[1], halves[0]), grid.partner())
        root = diagonal == number
        beside = (i ^ 1) + j == number
        held = jnp.where(root, mine, jnp.where(beside, given, jnp.zeros_like(mine)))
        for pairs in grid.tree(number):
            held = held + send(held, pairs)
        other = send(held, grid.partner())
        return jnp.concatenate(
            [jnp.where(even, held, other), jnp.where(even, other, held)], axis=0
        )

    def taken(parts, number):
        return lax.dynamic_index_in_dim(parts, jnp.clip(number - i, 0, cols - 1), 0, keepdims=False)

    def to_all(piece):
        return jnp.broadcast_to(piece, (cols, strip, width))

    solved = [solve(work)]
    sent = [solved[0].astype(half_type)]
    hop_down = send(sent[0], grid.moved(first, 1, 0))
    hop_right = send(sent[0], grid.moved(first, 0, 1))
    second = exchange(jnp.concatenate([a_strips[1], strips(sent[0])], axis=1), "col")
    a_full.append(whole(second[:, :strip]))
    piece = taken(second[:, strip:], first)
    far_down = send(sent[0], grid.moved(first, 2, 0))
    far_right = send(sent[0], grid.moved(first, 0, 2))
    down = [spread_deep(sent[0], first)]

    source = work - narrow(a_full[0], hop_down) - narrow(hop_right, b_full[0])
    solved.append(solve(source))
    sent.append(solved[1].astype(half_type))
    hop_down = send(sent[1], grid.moved(first + 1, 1, 0))
    hop_right = send(sent[1], grid.moved(first + 1, 0, 1))
    third = exchange(jnp.concatenate([to_all(piece), strips(sent[1])], axis=1), "col")
    across = [whole(third[:, :strip])]
    piece = taken(third[:, strip:], first + 1)
    a_full.append(
        send(
            a_full[1],
            grid.every(lambda k, l: (k, (l + 1) % cols), lambda k, l: k + l > last),
        )
    )
    down.append(spread_deep(sent[1], first + 1))

    source = (
        work
        - narrow(a_full[0], far_down)
        - narrow(far_right, b_full[0])
        - narrow(a_full[1], hop_down)
        - narrow(hop_right, b_full[1])
    )
    solved.append(solve(source))
    sent.append(solved[2].astype(half_type))
    fourth = exchange(jnp.concatenate([to_all(piece), strips(sent[2])], axis=1), "col")
    across.append(whole(fourth[:, :strip]))
    piece = taken(fourth[:, strip:], last)
    down.append(spread_deep(sent[2], last))
    across.append(whole(exchange(to_all(piece), "col")))

    behind = work
    for n in range(FRONTS):
        row_part = jnp.where(i <= first + n, across[n], jnp.zeros_like(across[n]))
        behind = behind - narrow(a_full[n], down[n]) - narrow(row_part, b_full[n])
    result = jnp.where(diagonal > last, behind, work)
    for n in range(FRONTS):
        result = jnp.where(diagonal == first + n, solved[n], result)
    return result


def solution(mesh):
    placed = (
        P("row", "col"),
        P("row", None, "col", None),
        P(None, "col", "row", None),
        P("row", None, "col", None),
        P("col", None, "row", None),
        P(),
    )
    return jax.shard_map(
        per_device, mesh=mesh, in_specs=placed, out_specs=P("row", "col"), check_vma=False
    )
```

```python
import functools

import jax
import jax.numpy as jnp
import numpy as np
from jax import lax
from jax.experimental import pallas as pl
from jax.experimental.pallas import tpu as pltpu
from jax.sharding import PartitionSpec as P


FRONTS = 3
CORES = 2
INTERPRET = False
PLACE = pltpu.HBM

half_type = jnp.bfloat16
full_type = jnp.float32


class Grid:
    def __init__(self, rows, cols):
        self.rows, self.cols, self.deep = rows, cols, rows // CORES

    def place(self, i, j):
        return i * self.cols + j

    def front(self, number):
        return [(i, number - i) for i in range(self.rows) if 0 <= number - i < self.cols]

    def moved(self, number, down, right):
        return [
            (self.place(i, j), self.place(i + down, j + right))
            for i, j in self.front(number)
            if i + down < self.rows and j + right < self.cols
        ]

    def every(self, target_of, wanted):
        pairs = []
        for i in range(self.rows):
            for j in range(self.cols):
                k, l = target_of(i, j)
                if wanted(k, l):
                    pairs.append((self.place(i, j), self.place(k, l)))
        return pairs

    def deeper(self, step, wanted):
        return self.every(lambda i, j: ((i + CORES * step) % self.rows, j), wanted)

    def partner(self):
        return self.every(lambda i, j: (i ^ 1, j), lambda i, j: True)

    def tree(self, number, behind):
        steps = [[] for _ in range(self.deep.bit_length() - 1)]
        for i, j in self.front(number):
            root = i // CORES
            lowest = (behind - j + 1) // CORES
            for core in range(CORES):
                sign = 1 if core == 0 else -1

                def reach(at, level):
                    size = self.deep >> (level + 1)
                    if size == 0:
                        return at != root and at >= lowest
                    there = (at + sign * size) % self.deep
                    one = reach(at, level + 1)
                    return reach(there, level + 1) or one

                def walk(at, level):
                    size = self.deep >> (level + 1)
                    if size == 0:
                        return
                    there = (at + sign * size) % self.deep
                    if reach(there, level + 1):
                        steps[level].append(
                            (self.place(CORES * at + core, j), self.place(CORES * there + core, j))
                        )
                        walk(there, level + 1)
                    walk(at, level + 1)

                walk(root, 0)
        return steps


def exchange(array, axis):
    return lax.all_to_all(array, axis, split_axis=0, concat_axis=0, tiled=True)


def send(array, pairs):
    return lax.ppermute(array, ("row", "col"), pairs)


LOCAL = []


def settled(array):
    if any(array is one for one in LOCAL):
        return pltpu.with_memory_space_constraint(array, PLACE)
    return array


def kernel(body, outs, *operands, scalars=(), scratch=(), late=()):
    operands = [one if isinstance(one, tuple) else (one, None) for one in operands]
    parts = [
        (8, 128)
        if part == "raw"
        else one.shape if part is None else np.empty(one.shape, np.bool_)[part].shape
        for one, part in operands
    ]
    many, most = len(operands), 24

    def run(*refs):
        refs = list(refs)

        def take(count):
            taken, refs[:count] = refs[:count], []
            return taken

        given, inputs, results = take(len(scalars)), take(many), take(len(outs))
        held, made, (arrival, departure) = take(many), take(len(outs)), take(2)
        copies = []
        begun, waited, started = set(), set(), []
        for k, (one, part) in enumerate(operands):
            source = inputs[k] if part is None or part == "raw" else inputs[k].at[part]
            copies.append(
                None if part == "raw" else pltpu.make_async_copy(source, held[k], arrival.at[k])
            )

        def begin(k):
            if k not in begun:
                copies[k].start()
                begun.add(k)

        def load(k):
            if copies[k] is None:
                return inputs[k]
            begin(k)
            if k not in waited:
                copies[k].wait()
                waited.add(k)
            return held[k]

        load.begin = begin
        for k in range(many):
            if k not in late and copies[k] is not None:
                begin(k)

        def store(k, part=None):
            source, target = made[k], results[k]
            if part is not None:
                source, target = source.at[part], target.at[part]
            started.append(pltpu.make_async_copy(source, target, departure.at[len(started)]))
            started[-1].start()

        body(given, load, made, store, *refs)
        for k in range(many):
            load(k)
        for copy in started:
            copy.wait()

    made_here = pl.pallas_call(
        run,
        out_shape=[PLACE(shape, kind) for shape, kind in outs],
        in_specs=[pl.BlockSpec(memory_space=pltpu.SMEM)] * len(scalars)
        + [pl.BlockSpec(memory_space=pl.ANY)] * many,
        out_specs=[pl.BlockSpec(memory_space=PLACE)] * len(outs),
        scratch_shapes=[
            *(pltpu.VMEM(part, one.dtype) for part, (one, _) in zip(parts, operands)),
            *(pltpu.VMEM(shape, kind) for shape, kind in outs),
            pltpu.SemaphoreType.DMA((many,)),
            pltpu.SemaphoreType.DMA((most,)),
            *scratch,
        ],
        compiler_params=pltpu.CompilerParams(vmem_limit_bytes=48 * 1024 * 1024),
        interpret=INTERPRET,
    )(*scalars, *(settled(one) for one, _ in operands))
    LOCAL.extend(made_here)
    return made_here


def split(values):
    high = values.astype(half_type)
    return high, (values - high.astype(full_type)).astype(half_type)


def narrow(left_side, right_side):
    return jnp.dot(left_side, right_side, preferred_element_type=full_type)


def thrice(left_high, left_low, right_high, right_low):
    return (
        narrow(left_high, right_low)
        + narrow(left_low, right_high)
        + narrow(left_high, right_high)
    )


def lower_times(low_tri, values):
    middle = low_tri[0].shape[0] // 2
    high, low = split(values)
    top = thrice(
        low_tri[0][:middle, :middle], low_tri[1][:middle, :middle], high[:middle], low[:middle]
    )
    bottom = thrice(low_tri[0][middle:], low_tri[1][middle:], high, low)
    return jnp.concatenate([top, bottom], axis=0)


def times_upper(values, upp_tri):
    middle = upp_tri[0].shape[0] // 2
    high, low = split(values)
    left = thrice(
        high[:, :middle], low[:, :middle], upp_tri[0][:middle, :middle], upp_tri[1][:middle, :middle]
    )
    right = thrice(high, low, upp_tri[0][:, middle:], upp_tri[1][:, middle:])
    return jnp.concatenate([left, right], axis=1)


def solve(source, u_pair, v_pair, scale, u_more, v_more, solved_ref):
    right = source - lower_times(u_pair, source)
    solved_ref[...] = (right - times_upper(right, v_pair)) * scale
    moved = lower_times(u_pair, solved_ref[...])
    solved_ref[...] += times_upper(moved, v_pair)
    u_ref, v_ref = u_more(), v_more()

    def doubled(power, carry):
        moved = lower_times((u_ref[power, 0], u_ref[power, 1]), solved_ref[...])
        solved_ref[...] += times_upper(moved, (v_ref[power, 0], v_ref[power, 1]))
        return carry

    lax.fori_loop(0, 2, doubled, 0)


def opening_body(shape, scalars, load, made, store):
    first, rows, cols, deep, strip = shape
    (at,) = scalars
    out_ref, v_out, *b_outs = made
    u_ref = load(0)
    high, low = split(u_ref[0])
    a_ref = load(1)
    for c in range(cols):
        out_ref[c, :strip] = high
        out_ref[c, strip : 2 * strip] = low
        for n in range(FRONTS):
            out_ref[c, (2 + n) * strip : (3 + n) * strip] = a_ref[0, (first + n - c) % cols]
    store(0)
    high, low = split(load(2)[0])
    v_out[:strip] = high
    v_out[strip:] = low
    store(1)
    b_ref = load(3)
    for step in range(deep):
        there = (at[0] + step) % deep
        for k in range(FRONTS + 1):
            tile = (first + FRONTS - 1 - k - CORES * there + rows) % rows
            b_outs[step][k * strip : (k + 1) * strip] = b_ref[tile, 0]
        store(2 + step)


def sorted_v_body(deep, scalars, load, made, store):
    (at,) = scalars
    for step in range(deep):
        made[0][(at[0] - step + deep) % deep] = load(step)[...]
    store(0)


def sorted_b_body(deep, strip, scalars, load, made, store):
    (at,) = scalars
    keep_ref, give_ref = made
    core = at[1]
    for step in range(deep):
        source = (at[0] - step + deep) % deep
        ref = load(step)
        for n in range(FRONTS):
            k = FRONTS - 1 - n
            keep_ref[n, source] = ref[pl.ds((k + core) * strip, strip)]
            give_ref[n, source] = ref[pl.ds((k + 1 - core) * strip, strip)]
    store(1)
    store(0)


def joined(scr, core, keep_ref, got_ref):
    deep, _, width = keep_ref.shape
    for z in range(deep):
        scr[CORES * z + core] = keep_ref[z]
        scr[CORES * z + 1 - core] = got_ref[z]
    return scr[...].reshape(width, width)


def square_of(ref):
    return ref[...].reshape(ref.shape[-1], ref.shape[-1])


def first_body(shape, scalars, load, made, store, v_scr):
    deep, strip, width = shape
    at, scale = scalars
    u_ref, v_ref, solved_ref, sent_ref = made
    core = at[1]
    for z in range(deep):
        for part in range(2):
            rows = slice(part * strip, (part + 1) * strip)
            v_scr[part, CORES * z + core] = load(0)[z, rows]
            v_scr[part, CORES * z + 1 - core] = load(1)[z, rows]
    for part in range(2):
        v_ref[0, part] = v_scr[part].reshape(width, width)
        u_ref[0, part] = load(2)[:, part * strip : (part + 1) * strip].reshape(width, width)
    store(0, 0)
    store(1, 0)

    def squared(power, carry):
        base = (u_ref[power, 0], u_ref[power, 1])
        value = base[0].astype(full_type) + base[1].astype(full_type)
        u_ref[power + 1, 0], u_ref[power + 1, 1] = split(lower_times(base, value))
        base = (v_ref[power, 0], v_ref[power, 1])
        value = base[0].astype(full_type) + base[1].astype(full_type)
        v_ref[power + 1, 0], v_ref[power + 1, 1] = split(times_upper(value, base))
        return carry

    lax.fori_loop(0, 2, squared, 0)
    for power in (1, 2):
        store(0, power)
        store(1, power)
    solve(
        load(3)[...], (u_ref[0, 0], u_ref[0, 1]), (v_ref[0, 0], v_ref[0, 1]), scale[0],
        lambda: u_ref.at[1:], lambda: v_ref.at[1:], solved_ref,
    )
    sent_ref[...] = solved_ref[...].astype(half_type)
    store(3)
    store(2)


def next_body(count, scalars, load, made, store, b_scr):
    at, scale = scalars
    solved_ref, sent_ref, mine_ref, give_ref = made[:4]
    width = solved_ref.shape[0]
    half = width // 2
    core, root = at[1], at[6]
    base = 3 + 5 * count
    source = load(2)[...]
    for n in range(count):
        a_at, down_at, right_at, keep_at, got_at = range(3 + 5 * n, 8 + 5 * n)
        source = source - narrow(square_of(load(a_at)), load(down_at)[...])
        b_tile = joined(b_scr, core, load(keep_at), load(got_at))
        source = source - narrow(load(right_at)[...], b_tile)
    load.begin(base)
    load.begin(base + 1)
    u_ref, v_ref = load(0), load(1)
    solve(
        source, (u_ref[0], u_ref[1]), (v_ref[0], v_ref[1]), scale[0],
        lambda: load(base), lambda: load(base + 1), solved_ref,
    )
    sent_ref[...] = solved_ref[...].astype(half_type)
    store(1)
    tiles = [sent_ref] if mine_ref.shape[0] == 1 else [load(4), sent_ref]
    for n, tile in enumerate(tiles):

        @pl.when(root > 0)
        def _():
            mine_ref[n] = tile[pl.ds(core * half, half)]
            give_ref[n] = tile[pl.ds((1 - core) * half, half)]

        @pl.when(root == 0)
        def _():
            mine_ref[n] = jnp.zeros((half, width), half_type)
            give_ref[n] = jnp.zeros((half, width), half_type)

    if len(made) > 4:
        cols, twice, _ = made[4].shape
        strip = twice // 2
        made[4][:, :strip] = load(5)[...].reshape(cols, strip, width)
        made[4][:, strip:] = sent_ref[...].reshape(cols, strip, width)
        store(4)
    store(3)
    store(2)
    store(0)


def packed_body(scalars, load, made, store, piece, arrival):
    (at,) = scalars
    (out_ref,) = made
    cols, thrice_strip, _ = out_ref.shape
    strip = thrice_strip // 3
    come = pltpu.make_async_copy(load(0).at[at[2]], piece, arrival.at[0])
    come.start()
    out_ref[:, 2 * strip :] = load(1)[...].reshape(cols, strip, -1)
    come.wait()
    out_ref[:, : 2 * strip] = jnp.broadcast_to(piece[...], (cols, *piece.shape))
    store(0)


def fanned_body(scalars, load, made, store, piece, arrival):
    (at,) = scalars
    strip = piece.shape[0]
    come = pltpu.make_async_copy(load(0).at[at[2], pl.ds(2 * strip, strip)], piece, arrival.at[0])
    come.start()
    come.wait()
    made[0][...] = jnp.broadcast_to(piece[...], made[0].shape)
    store(0)


def taken_off(n, at, load, total, base, b_scr, d_scr):
    a_at, held_at, other_at, right_at, keep_at, got_at = range(base, base + 6)
    core = at[1]
    half, width = d_scr.shape[1:]
    d_scr[core] = load(held_at)[...].reshape(half, width)
    d_scr[1 - core] = load(other_at)[...].reshape(half, width)
    total[...] -= narrow(square_of(load(a_at)), d_scr[...].reshape(width, width))
    b_tile = joined(b_scr, core, load(keep_at), load(got_at))
    row_part = square_of(load(right_at))

    @pl.when(at[3 + n] > 0)
    def _():
        total[...] -= narrow(row_part, b_tile)


def behind_body(scalars, load, made, store, b_scr, d_scr):
    (at,) = scalars
    (total,) = made
    total[...] = load(0)[...]
    for n in range(FRONTS):

        @pl.when(at[7] == n)
        def _(ref=load(1 + n)):
            total[...] = ref[...]

    for k in range(4, 16):
        load(k)

    @pl.when(at[7] == FRONTS)
    def _():
        for n in range(2):
            taken_off(n, at, load, total, 4 + 6 * n, b_scr, d_scr)

    store(0)


def behind_last_body(scalars, load, made, store, b_scr, d_scr):
    (at,) = scalars
    (total,) = made
    total[...] = load(0)[...]
    for k in range(1, 7):
        load(k)

    @pl.when(at[7] == FRONTS)
    def _():
        taken_off(2, at, load, total, 1, b_scr, d_scr)

    store(0)


def sweep(work, a_tiles, b_tiles, u_powers, v_powers, shift):
    LOCAL[:] = [work, a_tiles, b_tiles, u_powers, v_powers]
    rows = lax.axis_size("row")
    cols = lax.axis_size("col")
    grid = Grid(rows, cols)
    deep = grid.deep
    i = lax.axis_index("row")
    j = lax.axis_index("col")
    z, core = i // CORES, i % CORES
    diagonal = i + j
    first = max(0, (rows + cols) // 2 - FRONTS)
    last = first + FRONTS - 1
    width = work.shape[0]
    strip = width // cols
    half = width // 2
    tile = (width, width)
    scale = 0.5 / shift

    def place(number):
        kind = jnp.clip(diagonal - first, -1, FRONTS)
        return jnp.stack(
            [z, core, jnp.clip(number - i, 0, cols - 1)]
            + [(i <= first + n).astype(jnp.int32) for n in range(FRONTS)]
            + [(diagonal == number).astype(jnp.int32), kind]
        ).astype(jnp.int32)

    at, at_second, at_last = place(first), place(first + 1), place(last)
    near = {n: set() for n in range(cols)}
    for n in range(FRONTS):
        for r, c in grid.front(first + n):
            near[c].add(r // CORES)
    opening, v_mine, *b_mine = kernel(
        functools.partial(opening_body, (first, rows, cols, deep, strip)),
        [((cols, (2 + FRONTS) * strip, width), half_type), ((2 * strip, width), half_type)]
        + [(((FRONTS + 1) * strip, width), half_type)] * deep,
        (u_powers, (0, slice(0, 1))),
        a_tiles,
        (v_powers, (0, slice(0, 1))),
        b_tiles,
        scalars=(at,),
    )
    opened = exchange(opening, "col")
    v_all = [v_mine] + [
        send(v_mine, grid.deeper(s, lambda k, l: k // CORES in near[l]))
        for s in range(1, deep)
    ]
    b_all = [b_mine[0]] + [
        send(b_mine[s], grid.deeper(s, lambda k, l: k // CORES * CORES + CORES - 1 + l > first))
        for s in range(1, deep)
    ]
    (v_here,) = kernel(
        functools.partial(sorted_v_body, deep), [((deep, 2 * strip, width), half_type)],
        *v_all, scalars=(at,),
    )
    v_there = send(v_here, grid.partner())

    powers = ((3, 2, *tile), half_type)
    u_list, v_list, x_first, s_first = kernel(
        functools.partial(first_body, (deep, strip, width)),
        [powers, powers, (tile, full_type), (tile, half_type)],
        v_here, v_there, (opened, (slice(None), slice(0, 2 * strip))), work,
        scalars=(at, scale), scratch=[pltpu.VMEM((2, rows, strip, width), half_type)],
    )
    hop_down = send(s_first, grid.moved(first, 1, 0))
    hop_right = send(s_first, grid.moved(first, 0, 1))
    far_down = send(s_first, grid.moved(first, 2, 0))
    far_right = send(s_first, grid.moved(first, 0, 2))
    b_keep, b_give = kernel(
        functools.partial(sorted_b_body, deep, strip),
        [((FRONTS, deep, strip, width), half_type)] * 2, *b_all, scalars=(at,),
    )
    b_got = send(b_give, grid.partner())

    def a_of(n):
        return opened, (slice(None), slice((2 + n) * strip, (3 + n) * strip))

    b_scr = pltpu.VMEM((rows, strip, width), half_type)
    d_scr = pltpu.VMEM((2, half, width), half_type)
    more = [(u_list, slice(1, 3)), (v_list, slice(1, 3))]

    halves = ((1, half, width), half_type)
    both = ((2, half, width), half_type)
    x_second, s_second, t_mine, t_give, third_operand = kernel(
        functools.partial(next_body, 1),
        [(tile, full_type), (tile, half_type), both, both, ((cols, 2 * strip, width), half_type)],
        (u_list, 0), (v_list, 0), work, a_of(0), hop_down, hop_right, (b_keep, 0), (b_got, 0), *more,
        scalars=(at_second, scale), scratch=[b_scr], late=(8, 9),
    )
    hop_down = send(s_second, grid.moved(first + 1, 1, 0))
    hop_right = send(s_second, grid.moved(first + 1, 0, 1))
    third = exchange(third_operand, "col")

    x_third, s_third, l_mine, l_give = kernel(
        functools.partial(next_body, 2),
        [(tile, full_type), (tile, half_type), halves, halves],
        (u_list, 0), (v_list, 0), work,
        a_of(0), far_down, far_right, (b_keep, 0), (b_got, 0),
        a_of(1), hop_down, hop_right, (b_keep, 1), (b_got, 1), *more,
        scalars=(at_last, scale), scratch=[b_scr], late=(13, 14),
    )
    one = pltpu.SemaphoreType.DMA((1,))
    (fourth_operand,) = kernel(
        packed_body, [((cols, 3 * strip, width), half_type)], (third, "raw"), s_third,
        scalars=(at_second,), scratch=[pltpu.VMEM((2 * strip, width), half_type), one],
    )
    fourth = exchange(fourth_operand, "col")
    (fifth_operand,) = kernel(
        fanned_body, [((cols, strip, width), half_type)], (fourth, "raw"),
        scalars=(at_last,), scratch=[pltpu.VMEM((strip, width), half_type), one],
    )
    fifth = exchange(fifth_operand, "col")

    def spread_deep(mine, give, number):
        given = send(give, grid.partner())
        held = mine + given
        for pairs in grid.tree(number, last):
            got = send(held, pairs)
            held = held + got
        return held, send(held, grid.partner())

    t_held, t_other = spread_deep(t_mine, t_give, first + 1)
    l_held, l_other = spread_deep(l_mine, l_give, last)

    factors = []
    for n in range(2):
        factors += [
            a_of(n), (t_held, n), (t_other, n),
            (fourth, (slice(None), slice(n * strip, (n + 1) * strip))), (b_keep, n), (b_got, n),
        ]
    (behind,) = kernel(
        behind_body, [(tile, full_type)], work, x_first, x_second, x_third, *factors,
        scalars=(at,), scratch=[b_scr, d_scr],
    )
    (result,) = kernel(
        behind_last_body, [(tile, full_type)],
        behind, a_of(2), l_held, l_other, fifth, (b_keep, 2), (b_got, 2),
        scalars=(at,), scratch=[b_scr, d_scr],
    )
    return result


def solution(mesh):
    placed = (
        P("row", "col"),
        P("row", None, "col", None),
        P(None, "col", "row", None),
        P("row", None, "col", None),
        P("col", None, "row", None),
        P(),
    )
    return jax.shard_map(
        sweep, mesh=mesh, in_specs=placed, out_specs=P("row", "col"), check_vma=False
    )
```

```python
import functools

import jax
import jax.numpy as jnp
import numpy as np
from jax import lax
from jax.experimental import pallas as pl
from jax.experimental.pallas import tpu as pltpu
from jax.sharding import PartitionSpec as P


FRONTS = 3
CORES = 2
INTERPRET = False
PLACE = pltpu.HBM

half_type = jnp.bfloat16
full_type = jnp.float32


class Grid:
    def __init__(self, rows, cols):
        self.rows, self.cols, self.deep = rows, cols, rows // CORES

    def place(self, i, j):
        return i * self.cols + j

    def front(self, number):
        return [(i, number - i) for i in range(self.rows) if 0 <= number - i < self.cols]

    def moved(self, number, down, right):
        return [
            (self.place(i, j), self.place(i + down, j + right))
            for i, j in self.front(number)
            if i + down < self.rows and j + right < self.cols
        ]

    def every(self, target_of, wanted):
        pairs = []
        for i in range(self.rows):
            for j in range(self.cols):
                k, l = target_of(i, j)
                if wanted(k, l):
                    pairs.append((self.place(i, j), self.place(k, l)))
        return pairs

    def deeper(self, step, wanted):
        return self.every(lambda i, j: ((i + CORES * step) % self.rows, j), wanted)

    def partner(self):
        return self.every(lambda i, j: (i ^ 1, j), lambda i, j: True)

    def tree(self, number, behind):
        steps = [[] for _ in range(self.deep.bit_length() - 1)]
        for i, j in self.front(number):
            root = i // CORES
            lowest = (behind - j + 1) // CORES
            for core in range(CORES):
                sign = 1 if core == 0 else -1

                def reach(at, level):
                    size = self.deep >> (level + 1)
                    if size == 0:
                        return at != root and at >= lowest
                    there = (at + sign * size) % self.deep
                    one = reach(at, level + 1)
                    return reach(there, level + 1) or one

                def walk(at, level):
                    size = self.deep >> (level + 1)
                    if size == 0:
                        return
                    there = (at + sign * size) % self.deep
                    if reach(there, level + 1):
                        steps[level].append(
                            (self.place(CORES * at + core, j), self.place(CORES * there + core, j))
                        )
                        walk(there, level + 1)
                    walk(at, level + 1)

                walk(root, 0)
        return steps


def exchange(array, axis):
    return lax.all_to_all(array, axis, split_axis=0, concat_axis=0, tiled=True)


def send(array, pairs):
    return lax.ppermute(array, ("row", "col"), pairs)


LOCAL = []


def settled(array):
    if any(array is one for one in LOCAL):
        return pltpu.with_memory_space_constraint(array, PLACE)
    return array


def kernel(body, outs, *operands, scalars=(), scratch=(), late=()):
    operands = [one if isinstance(one, tuple) else (one, None) for one in operands]
    parts = [
        (8, 128)
        if part == "raw"
        else one.shape if part is None else np.empty(one.shape, np.bool_)[part].shape
        for one, part in operands
    ]
    many, most = len(operands), 24

    def run(*refs):
        refs = list(refs)

        def take(count):
            taken, refs[:count] = refs[:count], []
            return taken

        given, inputs, results = take(len(scalars)), take(many), take(len(outs))
        held, made, (arrival, departure) = take(many), take(len(outs)), take(2)
        copies = []
        begun, waited, started = set(), set(), []
        for k, (one, part) in enumerate(operands):
            source = inputs[k] if part is None or part == "raw" else inputs[k].at[part]
            copies.append(
                None if part == "raw" else pltpu.make_async_copy(source, held[k], arrival.at[k])
            )

        def begin(k):
            if k not in begun:
                copies[k].start()
                begun.add(k)

        def load(k):
            if copies[k] is None:
                return inputs[k]
            begin(k)
            if k not in waited:
                copies[k].wait()
                waited.add(k)
            return held[k]

        load.begin = begin
        for k in range(many):
            if k not in late and copies[k] is not None:
                begin(k)

        def store(k, part=None):
            source, target = made[k], results[k]
            if part is not None:
                source, target = source.at[part], target.at[part]
            started.append(pltpu.make_async_copy(source, target, departure.at[len(started)]))
            started[-1].start()

        body(given, load, made, store, *refs)
        for k in range(many):
            load(k)
        for copy in started:
            copy.wait()

    made_here = pl.pallas_call(
        run,
        out_shape=[PLACE(shape, kind) for shape, kind in outs],
        in_specs=[pl.BlockSpec(memory_space=pltpu.SMEM)] * len(scalars)
        + [pl.BlockSpec(memory_space=pl.ANY)] * many,
        out_specs=[pl.BlockSpec(memory_space=PLACE)] * len(outs),
        scratch_shapes=[
            *(pltpu.VMEM(part, one.dtype) for part, (one, _) in zip(parts, operands)),
            *(pltpu.VMEM(shape, kind) for shape, kind in outs),
            pltpu.SemaphoreType.DMA((many,)),
            pltpu.SemaphoreType.DMA((most,)),
            *scratch,
        ],
        compiler_params=pltpu.CompilerParams(vmem_limit_bytes=48 * 1024 * 1024),
        interpret=INTERPRET,
    )(*scalars, *(settled(one) for one, _ in operands))
    LOCAL.extend(made_here)
    return made_here


def split(values):
    high = values.astype(half_type)
    return high, (values - high.astype(full_type)).astype(half_type)


def narrow(left_side, right_side):
    return jnp.dot(left_side, right_side, preferred_element_type=full_type)


def thrice(left_high, left_low, right_high, right_low):
    return (
        narrow(left_high, right_low)
        + narrow(left_low, right_high)
        + narrow(left_high, right_high)
    )


def lower_times(low_tri, values):
    middle = low_tri[0].shape[0] // 2
    high, low = split(values)
    top = thrice(
        low_tri[0][:middle, :middle], low_tri[1][:middle, :middle], high[:middle], low[:middle]
    )
    bottom = thrice(low_tri[0][middle:], low_tri[1][middle:], high, low)
    return jnp.concatenate([top, bottom], axis=0)


def times_upper(values, upp_tri):
    middle = upp_tri[0].shape[0] // 2
    high, low = split(values)
    left = thrice(
        high[:, :middle], low[:, :middle], upp_tri[0][:middle, :middle], upp_tri[1][:middle, :middle]
    )
    right = thrice(high, low, upp_tri[0][:, middle:], upp_tri[1][:, middle:])
    return jnp.concatenate([left, right], axis=1)


def doubled(u_ref, v_ref, solved_ref):
    def once(power, carry):
        moved = lower_times((u_ref[power, 0], u_ref[power, 1]), solved_ref[...])
        solved_ref[...] += times_upper(moved, (v_ref[power, 0], v_ref[power, 1]))
        return carry

    lax.fori_loop(0, 2, once, 0)


def begun(source, u_pair, v_pair, scale, solved_ref):
    right = source - lower_times(u_pair, source)
    solved_ref[...] = (right - times_upper(right, v_pair)) * scale
    moved = lower_times(u_pair, solved_ref[...])
    solved_ref[...] += times_upper(moved, v_pair)


def opening_body(shape, scalars, load, made, store):
    first, rows, cols, deep, strip = shape
    (at,) = scalars
    out_ref, v_out, *b_outs = made
    u_ref = load(0)
    high, low = split(u_ref[0])
    a_ref = load(1)
    for c in range(cols):
        out_ref[c, :strip] = high
        out_ref[c, strip : 2 * strip] = low
        for n in range(FRONTS):
            out_ref[c, (2 + n) * strip : (3 + n) * strip] = a_ref[0, (first + n - c) % cols]
    store(0)
    high, low = split(load(2)[0])
    v_out[:strip] = high
    v_out[strip:] = low
    store(1)
    b_ref = load(3)
    for step in range(deep):
        there = (at[0] + step) % deep
        for k in range(FRONTS + 1):
            tile = (first + FRONTS - 1 - k - CORES * there + rows) % rows
            b_outs[step][k * strip : (k + 1) * strip] = b_ref[tile, 0]
        store(2 + step)


def sorted_v_body(deep, scalars, load, made, store):
    (at,) = scalars
    for step in range(deep):
        made[0][(at[0] - step + deep) % deep] = load(step)[...]
    store(0)


def sorted_b_body(deep, strip, scalars, load, made, store):
    (at,) = scalars
    keep_ref, give_ref = made
    core = at[1]
    for step in range(deep):
        source = (at[0] - step + deep) % deep
        ref = load(step)
        for n in range(FRONTS):
            k = FRONTS - 1 - n
            keep_ref[n, source] = ref[pl.ds((k + core) * strip, strip)]
            give_ref[n, source] = ref[pl.ds((k + 1 - core) * strip, strip)]
    store(1)
    store(0)


def joined(scr, core, keep_ref, got_ref):
    deep, _, width = keep_ref.shape
    for z in range(deep):
        scr[CORES * z + core] = keep_ref[z]
        scr[CORES * z + 1 - core] = got_ref[z]
    return scr[...].reshape(width, width)


def square_of(ref):
    return ref[...].reshape(ref.shape[-1], ref.shape[-1])


def first_body(shape, scalars, load, made, store, v_scr):
    deep, strip, width = shape
    at, scale = scalars
    u_ref, v_ref, solved_ref, sent_ref = made
    core = at[1]
    for z in range(deep):
        for part in range(2):
            rows = slice(part * strip, (part + 1) * strip)
            v_scr[part, CORES * z + core] = load(0)[z, rows]
            v_scr[part, CORES * z + 1 - core] = load(1)[z, rows]
    for part in range(2):
        v_ref[0, part] = v_scr[part].reshape(width, width)
        u_ref[0, part] = load(2)[:, part * strip : (part + 1) * strip].reshape(width, width)
    store(0, 0)
    store(1, 0)

    def squared(power, carry):
        base = (u_ref[power, 0], u_ref[power, 1])
        value = base[0].astype(full_type) + base[1].astype(full_type)
        u_ref[power + 1, 0], u_ref[power + 1, 1] = split(lower_times(base, value))
        base = (v_ref[power, 0], v_ref[power, 1])
        value = base[0].astype(full_type) + base[1].astype(full_type)
        v_ref[power + 1, 0], v_ref[power + 1, 1] = split(times_upper(value, base))
        return carry

    @pl.when((at[7] >= 0) & (at[7] < FRONTS))
    def _():
        lax.fori_loop(0, 2, squared, 0)

    for power in (1, 2):
        store(0, power)
        store(1, power)
    source = load(3)[...]

    @pl.when(at[6] > 0)
    def _():
        begun(source, (u_ref[0, 0], u_ref[0, 1]), (v_ref[0, 0], v_ref[0, 1]), scale[0], solved_ref)
        doubled(u_ref.at[1:], v_ref.at[1:], solved_ref)
        sent_ref[...] = solved_ref[...].astype(half_type)

    store(3)
    store(2)


def next_body(count, scalars, load, made, store, b_scr):
    at, scale = scalars
    solved_ref, sent_ref, mine_ref, give_ref = made[:4]
    width = solved_ref.shape[0]
    half = width // 2
    core, root = at[1], at[6]
    base = 3 + 5 * count
    for k in range(base):
        load(k)
    load.begin(base)
    load.begin(base + 1)
    u_ref, v_ref = load(0), load(1)

    @pl.when(root > 0)
    def _():
        source = load(2)[...]
        for n in range(count):
            a_at, down_at, right_at, keep_at, got_at = range(3 + 5 * n, 8 + 5 * n)
            source = source - narrow(square_of(load(a_at)), load(down_at)[...])
            b_tile = joined(b_scr.at[n], core, load(keep_at), load(got_at))
            source = source - narrow(load(right_at)[...], b_tile)
        begun(source, (u_ref[0], u_ref[1]), (v_ref[0], v_ref[1]), scale[0], solved_ref)

    u_high, v_high = load(base), load(base + 1)

    @pl.when(root > 0)
    def _():
        doubled(u_high, v_high, solved_ref)
        sent_ref[...] = solved_ref[...].astype(half_type)

    store(1)
    tiles = [sent_ref] if mine_ref.shape[0] == 1 else [load(4), sent_ref]
    for n, tile in enumerate(tiles):

        @pl.when(root > 0)
        def _():
            mine_ref[n] = tile[pl.ds(core * half, half)]
            give_ref[n] = tile[pl.ds((1 - core) * half, half)]

        @pl.when(root == 0)
        def _():
            mine_ref[n] = jnp.zeros((half, width), half_type)
            give_ref[n] = jnp.zeros((half, width), half_type)

    if len(made) > 4:
        cols, twice, _ = made[4].shape
        strip = twice // 2
        made[4][:, :strip] = load(5)[...].reshape(cols, strip, width)
        made[4][:, strip:] = sent_ref[...].reshape(cols, strip, width)
        store(4)
    store(3)
    store(2)
    store(0)


def packed_body(scalars, load, made, store, piece, arrival):
    (at,) = scalars
    (out_ref,) = made
    cols, thrice_strip, _ = out_ref.shape
    strip = thrice_strip // 3
    come = pltpu.make_async_copy(load(0).at[at[2]], piece, arrival.at[0])
    come.start()
    out_ref[:, 2 * strip :] = load(1)[...].reshape(cols, strip, -1)
    come.wait()
    out_ref[:, : 2 * strip] = jnp.broadcast_to(piece[...], (cols, *piece.shape))
    store(0)


def fanned_body(scalars, load, made, store, piece, arrival):
    (at,) = scalars
    strip = piece.shape[0]
    come = pltpu.make_async_copy(load(0).at[at[2], pl.ds(2 * strip, strip)], piece, arrival.at[0])
    come.start()
    come.wait()
    made[0][...] = jnp.broadcast_to(piece[...], made[0].shape)
    store(0)


def taken_off(n, at, load, total, base, b_scr, d_scr):
    a_at, held_at, other_at, right_at, keep_at, got_at = range(base, base + 6)
    core = at[1]
    half, width = d_scr.shape[1:]
    d_scr[core] = load(held_at)[...].reshape(half, width)
    d_scr[1 - core] = load(other_at)[...].reshape(half, width)
    total[...] -= narrow(square_of(load(a_at)), d_scr[...].reshape(width, width))
    b_tile = joined(b_scr, core, load(keep_at), load(got_at))
    row_part = square_of(load(right_at))

    @pl.when(at[3 + n] > 0)
    def _():
        total[...] -= narrow(row_part, b_tile)


def behind_body(scalars, load, made, store, b_scr, d_scr):
    (at,) = scalars
    (total,) = made
    total[...] = load(0)[...]
    for n in range(FRONTS):

        @pl.when(at[7] == n)
        def _(ref=load(1 + n)):
            total[...] = ref[...]

    for k in range(4, 16):
        load(k)

    @pl.when(at[7] == FRONTS)
    def _():
        for n in range(2):
            taken_off(n, at, load, total, 4 + 6 * n, b_scr.at[n], d_scr.at[n])

    store(0)


def behind_last_body(scalars, load, made, store, b_scr, d_scr):
    (at,) = scalars
    (total,) = made
    total[...] = load(0)[...]
    for k in range(1, 7):
        load(k)

    @pl.when(at[7] == FRONTS)
    def _():
        taken_off(2, at, load, total, 1, b_scr, d_scr)

    store(0)


def sweep(work, a_tiles, b_tiles, u_powers, v_powers, shift):
    LOCAL[:] = [work, a_tiles, b_tiles, u_powers, v_powers]
    rows = lax.axis_size("row")
    cols = lax.axis_size("col")
    grid = Grid(rows, cols)
    deep = grid.deep
    i = lax.axis_index("row")
    j = lax.axis_index("col")
    z, core = i // CORES, i % CORES
    diagonal = i + j
    first = max(0, (rows + cols) // 2 - FRONTS)
    last = first + FRONTS - 1
    width = work.shape[0]
    strip = width // cols
    half = width // 2
    tile = (width, width)
    scale = 0.5 / shift

    def place(number):
        kind = jnp.clip(diagonal - first, -1, FRONTS)
        return jnp.stack(
            [z, core, jnp.clip(number - i, 0, cols - 1)]
            + [(i <= first + n).astype(jnp.int32) for n in range(FRONTS)]
            + [(diagonal == number).astype(jnp.int32), kind]
        ).astype(jnp.int32)

    at, at_second, at_last = place(first), place(first + 1), place(last)
    near = {n: set() for n in range(cols)}
    for n in range(FRONTS):
        for r, c in grid.front(first + n):
            near[c].add(r // CORES)
    opening, v_mine, *b_mine = kernel(
        functools.partial(opening_body, (first, rows, cols, deep, strip)),
        [((cols, (2 + FRONTS) * strip, width), half_type), ((2 * strip, width), half_type)]
        + [(((FRONTS + 1) * strip, width), half_type)] * deep,
        (u_powers, (0, slice(0, 1))),
        a_tiles,
        (v_powers, (0, slice(0, 1))),
        b_tiles,
        scalars=(at,),
    )
    opened = exchange(opening, "col")
    v_all = [v_mine] + [
        send(v_mine, grid.deeper(s, lambda k, l: k // CORES in near[l]))
        for s in range(1, deep)
    ]
    b_all = [b_mine[0]] + [
        send(b_mine[s], grid.deeper(s, lambda k, l: k // CORES * CORES + CORES - 1 + l > first))
        for s in range(1, deep)
    ]
    (v_here,) = kernel(
        functools.partial(sorted_v_body, deep), [((deep, 2 * strip, width), half_type)],
        *v_all, scalars=(at,),
    )
    v_there = send(v_here, grid.partner())

    powers = ((3, 2, *tile), half_type)
    u_list, v_list, x_first, s_first = kernel(
        functools.partial(first_body, (deep, strip, width)),
        [powers, powers, (tile, full_type), (tile, half_type)],
        v_here, v_there, (opened, (slice(None), slice(0, 2 * strip))), work,
        scalars=(at, scale), scratch=[pltpu.VMEM((2, rows, strip, width), half_type)],
    )
    hop_down = send(s_first, grid.moved(first, 1, 0))
    hop_right = send(s_first, grid.moved(first, 0, 1))
    far_down = send(s_first, grid.moved(first, 2, 0))
    far_right = send(s_first, grid.moved(first, 0, 2))
    b_keep, b_give = kernel(
        functools.partial(sorted_b_body, deep, strip),
        [((FRONTS, deep, strip, width), half_type)] * 2, *b_all, scalars=(at,),
    )
    b_got = send(b_give, grid.partner())

    def a_of(n):
        return opened, (slice(None), slice((2 + n) * strip, (3 + n) * strip))

    b_scr = pltpu.VMEM((rows, strip, width), half_type)
    b_more = pltpu.VMEM((2, rows, strip, width), half_type)
    d_scr = pltpu.VMEM((2, half, width), half_type)
    more = [(u_list, slice(1, 3)), (v_list, slice(1, 3))]

    halves = ((1, half, width), half_type)
    both = ((2, half, width), half_type)
    x_second, s_second, t_mine, t_give, third_operand = kernel(
        functools.partial(next_body, 1),
        [(tile, full_type), (tile, half_type), both, both, ((cols, 2 * strip, width), half_type)],
        (u_list, 0), (v_list, 0), work, a_of(0), hop_down, hop_right, (b_keep, 0), (b_got, 0), *more,
        scalars=(at_second, scale), scratch=[b_more], late=(8, 9),
    )
    hop_down = send(s_second, grid.moved(first + 1, 1, 0))
    hop_right = send(s_second, grid.moved(first + 1, 0, 1))
    third = exchange(third_operand, "col")

    x_third, s_third, l_mine, l_give = kernel(
        functools.partial(next_body, 2),
        [(tile, full_type), (tile, half_type), halves, halves],
        (u_list, 0), (v_list, 0), work,
        a_of(0), far_down, far_right, (b_keep, 0), (b_got, 0),
        a_of(1), hop_down, hop_right, (b_keep, 1), (b_got, 1), *more,
        scalars=(at_last, scale), scratch=[b_more], late=(13, 14),
    )
    one = pltpu.SemaphoreType.DMA((1,))
    (fourth_operand,) = kernel(
        packed_body, [((cols, 3 * strip, width), half_type)], (third, "raw"), s_third,
        scalars=(at_second,), scratch=[pltpu.VMEM((2 * strip, width), half_type), one],
    )
    fourth = exchange(fourth_operand, "col")
    (fifth_operand,) = kernel(
        fanned_body, [((cols, strip, width), half_type)], (fourth, "raw"),
        scalars=(at_last,), scratch=[pltpu.VMEM((strip, width), half_type), one],
    )
    fifth = exchange(fifth_operand, "col")

    def spread_deep(mine, give, number):
        given = send(give, grid.partner())
        held = mine + given
        for pairs in grid.tree(number, last):
            got = send(held, pairs)
            held = held + got
        return held, send(held, grid.partner())

    t_held, t_other = spread_deep(t_mine, t_give, first + 1)
    l_held, l_other = spread_deep(l_mine, l_give, last)

    factors = []
    for n in range(2):
        factors += [
            a_of(n), (t_held, n), (t_other, n),
            (fourth, (slice(None), slice(n * strip, (n + 1) * strip))), (b_keep, n), (b_got, n),
        ]
    (behind,) = kernel(
        behind_body, [(tile, full_type)], work, x_first, x_second, x_third, *factors,
        scalars=(at,), scratch=[b_more, pltpu.VMEM((2, 2, half, width), half_type)],
    )
    (result,) = kernel(
        behind_last_body, [(tile, full_type)],
        behind, a_of(2), l_held, l_other, fifth, (b_keep, 2), (b_got, 2),
        scalars=(at,), scratch=[b_scr, d_scr],
    )
    return result


def solution(mesh):
    placed = (
        P("row", "col"),
        P("row", None, "col", None),
        P(None, "col", "row", None),
        P("row", None, "col", None),
        P("col", None, "row", None),
        P(),
    )
    return jax.shard_map(
        sweep, mesh=mesh, in_specs=placed, out_specs=P("row", "col"), check_vma=False
    )
```

```python
import functools

import jax
import jax.numpy as jnp
import numpy as np
from jax import lax
from jax.experimental import pallas as pl
from jax.experimental.pallas import tpu as pltpu
from jax.sharding import PartitionSpec as P


FRONTS = 3
CORES = 2
INTERPRET = False
PLACE = pltpu.HBM

half_type = jnp.bfloat16
full_type = jnp.float32


class Grid:
    def __init__(self, rows, cols):
        self.rows, self.cols, self.deep = rows, cols, rows // CORES

    def place(self, i, j):
        return i * self.cols + j

    def front(self, number):
        return [(i, number - i) for i in range(self.rows) if 0 <= number - i < self.cols]

    def moved(self, number, down, right):
        return [
            (self.place(i, j), self.place(i + down, j + right))
            for i, j in self.front(number)
            if i + down < self.rows and j + right < self.cols
        ]

    def every(self, target_of, wanted):
        pairs = []
        for i in range(self.rows):
            for j in range(self.cols):
                k, l = target_of(i, j)
                if wanted(k, l):
                    pairs.append((self.place(i, j), self.place(k, l)))
        return pairs

    def deeper(self, step, wanted):
        return self.every(lambda i, j: ((i + CORES * step) % self.rows, j), wanted)

    def partner(self):
        return self.every(lambda i, j: (i ^ 1, j), lambda i, j: True)

    def tree(self, number, behind):
        steps = [[] for _ in range(self.deep.bit_length() - 1)]
        for i, j in self.front(number):
            root = i // CORES
            lowest = (behind - j + 1) // CORES
            for core in range(CORES):
                sign = 1 if core == 0 else -1

                def reach(at, level):
                    size = self.deep >> (level + 1)
                    if size == 0:
                        return at != root and at >= lowest
                    there = (at + sign * size) % self.deep
                    one = reach(at, level + 1)
                    return reach(there, level + 1) or one

                def walk(at, level):
                    size = self.deep >> (level + 1)
                    if size == 0:
                        return
                    there = (at + sign * size) % self.deep
                    if reach(there, level + 1):
                        steps[level].append(
                            (self.place(CORES * at + core, j), self.place(CORES * there + core, j))
                        )
                        walk(there, level + 1)
                    walk(at, level + 1)

                walk(root, 0)
        return steps


def exchange(array, axis):
    return lax.all_to_all(array, axis, split_axis=0, concat_axis=0, tiled=True)


def send(array, pairs):
    return lax.ppermute(array, ("row", "col"), pairs)


LOCAL = []


def settled(array):
    if any(array is one for one in LOCAL):
        return pltpu.with_memory_space_constraint(array, PLACE)
    return array


def kernel(body, outs, *operands, scalars=(), scratch=(), late=(), when=None, other=None):
    operands = [one if isinstance(one, tuple) else (one, None) for one in operands]
    parts = [
        (8, 128)
        if part == "raw"
        else one.shape if part is None else np.empty(one.shape, np.bool_)[part].shape
        for one, part in operands
    ]
    many, most = len(operands), 24

    def run(*refs):
        refs = list(refs)

        def take(count):
            taken, refs[:count] = refs[:count], []
            return taken

        given, inputs, results = take(len(scalars)), take(many), take(len(outs))
        held, made, (arrival, departure) = take(many), take(len(outs)), take(2)

        def act(work, idle=False):
            copies, begun, waited, started = [], set(), set(), []
            for k, (one, part) in enumerate(operands):
                if part == "raw":
                    copies.append(None)
                    continue
                source = inputs[k] if part is None else inputs[k].at[part]
                copies.append(pltpu.make_async_copy(source, held[k], arrival.at[k]))

            def begin(k):
                if k not in begun:
                    copies[k].start()
                    begun.add(k)

            def load(k):
                if copies[k] is None:
                    return inputs[k]
                begin(k)
                if k not in waited:
                    copies[k].wait()
                    waited.add(k)
                return held[k]

            def store(k, part=None):
                source, target = made[k], results[k]
                if part is not None:
                    source, target = source.at[part], target.at[part]
                started.append(pltpu.make_async_copy(source, target, departure.at[len(started)]))
                started[-1].start()

            load.begin = begin
            if not idle:
                for k in range(many):
                    if k not in late and copies[k] is not None:
                        begin(k)
            work(given, load, made, store, *refs)
            if not idle:
                for k in range(many):
                    load(k)
            for copy in started:
                copy.wait()

        if when is None:
            act(body)
            return
        pl.when(when(given))(lambda: act(body))
        if other is not None:
            pl.when(jnp.logical_not(when(given)))(lambda: act(other, True))

    made_here = pl.pallas_call(
        run,
        out_shape=[PLACE(shape, kind) for shape, kind in outs],
        in_specs=[pl.BlockSpec(memory_space=pltpu.SMEM)] * len(scalars)
        + [pl.BlockSpec(memory_space=pl.ANY)] * many,
        out_specs=[pl.BlockSpec(memory_space=PLACE)] * len(outs),
        scratch_shapes=[
            *(pltpu.VMEM(part, one.dtype) for part, (one, _) in zip(parts, operands)),
            *(pltpu.VMEM(shape, kind) for shape, kind in outs),
            pltpu.SemaphoreType.DMA((many,)),
            pltpu.SemaphoreType.DMA((most,)),
            *scratch,
        ],
        compiler_params=pltpu.CompilerParams(vmem_limit_bytes=48 * 1024 * 1024),
        interpret=INTERPRET,
    )(*scalars, *(settled(one) for one, _ in operands))
    LOCAL.extend(made_here)
    return made_here


def split(values):
    high = values.astype(half_type)
    return high, (values - high.astype(full_type)).astype(half_type)


def narrow(left_side, right_side):
    return jnp.dot(left_side, right_side, preferred_element_type=full_type)


def thrice(left_high, left_low, right_high, right_low):
    return (
        narrow(left_high, right_low)
        + narrow(left_low, right_high)
        + narrow(left_high, right_high)
    )


def lower_times(low_tri, values):
    middle = low_tri[0].shape[0] // 2
    high, low = split(values)
    top = thrice(
        low_tri[0][:middle, :middle], low_tri[1][:middle, :middle], high[:middle], low[:middle]
    )
    bottom = thrice(low_tri[0][middle:], low_tri[1][middle:], high, low)
    return jnp.concatenate([top, bottom], axis=0)


def times_upper(values, upp_tri):
    middle = upp_tri[0].shape[0] // 2
    high, low = split(values)
    left = thrice(
        high[:, :middle], low[:, :middle], upp_tri[0][:middle, :middle], upp_tri[1][:middle, :middle]
    )
    right = thrice(high, low, upp_tri[0][:, middle:], upp_tri[1][:, middle:])
    return jnp.concatenate([left, right], axis=1)


def doubled(u_ref, v_ref, solved_ref):
    def once(power, carry):
        moved = lower_times((u_ref[power, 0], u_ref[power, 1]), solved_ref[...])
        solved_ref[...] += times_upper(moved, (v_ref[power, 0], v_ref[power, 1]))
        return carry

    lax.fori_loop(0, 2, once, 0)


def begun(source, u_pair, v_pair, scale, solved_ref):
    right = source - lower_times(u_pair, source)
    solved_ref[...] = (right - times_upper(right, v_pair)) * scale
    moved = lower_times(u_pair, solved_ref[...])
    solved_ref[...] += times_upper(moved, v_pair)


def opening_body(shape, scalars, load, made, store):
    first, rows, cols, deep, strip = shape
    (at,) = scalars
    out_ref, v_out, *b_outs = made
    u_ref = load(0)
    high, low = split(u_ref[0])
    a_ref = load(1)
    for c in range(cols):
        out_ref[c, :strip] = high
        out_ref[c, strip : 2 * strip] = low
        for n in range(FRONTS):
            out_ref[c, (2 + n) * strip : (3 + n) * strip] = a_ref[0, (first + n - c) % cols]
    store(0)
    high, low = split(load(2)[0])
    v_out[:strip] = high
    v_out[strip:] = low
    store(1)
    b_ref = load(3)
    for step in range(deep):
        there = (at[0] + step) % deep
        for k in range(FRONTS + 1):
            tile = (first + FRONTS - 1 - k - CORES * there + rows) % rows
            b_outs[step][k * strip : (k + 1) * strip] = b_ref[tile, 0]
        store(2 + step)


def sorted_v_body(deep, scalars, load, made, store):
    (at,) = scalars
    for step in range(deep):
        made[0][(at[0] - step + deep) % deep] = load(step)[...]
    store(0)


def sorted_b_body(deep, strip, scalars, load, made, store):
    (at,) = scalars
    keep_ref, give_ref = made
    core = at[1]
    for step in range(deep):
        source = (at[0] - step + deep) % deep
        ref = load(step)
        for n in range(FRONTS):
            k = FRONTS - 1 - n
            keep_ref[n, source] = ref[pl.ds((k + core) * strip, strip)]
            give_ref[n, source] = ref[pl.ds((k + 1 - core) * strip, strip)]
    store(1)
    store(0)


def joined(scr, core, keep_ref, got_ref):
    deep, _, width = keep_ref.shape
    for z in range(deep):
        scr[CORES * z + core] = keep_ref[z]
        scr[CORES * z + 1 - core] = got_ref[z]
    return scr[...].reshape(width, width)


def square_of(ref):
    return ref[...].reshape(ref.shape[-1], ref.shape[-1])


def first_body(shape, scalars, load, made, store, v_scr):
    deep, strip, width = shape
    at, scale = scalars
    u_ref, v_ref, solved_ref, sent_ref = made
    core = at[1]
    for z in range(deep):
        for part in range(2):
            rows = slice(part * strip, (part + 1) * strip)
            v_scr[part, CORES * z + core] = load(0)[z, rows]
            v_scr[part, CORES * z + 1 - core] = load(1)[z, rows]
    for part in range(2):
        v_ref[0, part] = v_scr[part].reshape(width, width)
        u_ref[0, part] = load(2)[:, part * strip : (part + 1) * strip].reshape(width, width)
    store(0, 0)
    store(1, 0)

    def squared(power, carry):
        base = (u_ref[power, 0], u_ref[power, 1])
        value = base[0].astype(full_type) + base[1].astype(full_type)
        u_ref[power + 1, 0], u_ref[power + 1, 1] = split(lower_times(base, value))
        base = (v_ref[power, 0], v_ref[power, 1])
        value = base[0].astype(full_type) + base[1].astype(full_type)
        v_ref[power + 1, 0], v_ref[power + 1, 1] = split(times_upper(value, base))
        return carry

    lax.fori_loop(0, 2, squared, 0)
    for power in (1, 2):
        store(0, power)
        store(1, power)
    source = load(3)[...]

    @pl.when(at[6] > 0)
    def _():
        begun(source, (u_ref[0, 0], u_ref[0, 1]), (v_ref[0, 0], v_ref[0, 1]), scale[0], solved_ref)
        doubled(u_ref.at[1:], v_ref.at[1:], solved_ref)
        sent_ref[...] = solved_ref[...].astype(half_type)

    store(3)
    store(2)


def next_body(count, scalars, load, made, store, b_scr):
    at, scale = scalars
    solved_ref, sent_ref, mine_ref, give_ref = made[:4]
    width = solved_ref.shape[0]
    half = width // 2
    core = at[1]
    base = 3 + 5 * count
    for k in range(2, base):
        load(k)
    load.begin(base)
    load.begin(base + 1)
    source = load(2)[...]
    for n in range(count):
        a_at, down_at, right_at, keep_at, got_at = range(3 + 5 * n, 8 + 5 * n)
        source = source - narrow(square_of(load(a_at)), load(down_at)[...])
        b_tile = joined(b_scr.at[n], core, load(keep_at), load(got_at))
        source = source - narrow(load(right_at)[...], b_tile)
    u_ref, v_ref = load(0), load(1)
    begun(source, (u_ref[0], u_ref[1]), (v_ref[0], v_ref[1]), scale[0], solved_ref)
    doubled(load(base), load(base + 1), solved_ref)
    sent_ref[...] = solved_ref[...].astype(half_type)
    store(1)
    store(0)
    tiles = [sent_ref] if mine_ref.shape[0] == 1 else [load(4), sent_ref]
    for n, tile in enumerate(tiles):
        mine_ref[n] = tile[pl.ds(core * half, half)]
        give_ref[n] = tile[pl.ds((1 - core) * half, half)]
    if len(made) > 4:
        cols, twice, _ = made[4].shape
        strip = twice // 2
        made[4][:, :strip] = load(5)[...].reshape(cols, strip, width)
        made[4][:, strip:] = sent_ref[...].reshape(cols, strip, width)
        store(4)
    store(3)
    store(2)


def nothing_sent(scalars, load, made, store, b_scr):
    for k in (2, 3):
        made[k][...] = jnp.zeros(made[k].shape, half_type)
        store(k)


def packed_body(scalars, load, made, store, piece, arrival):
    (at,) = scalars
    (out_ref,) = made
    cols, thrice_strip, _ = out_ref.shape
    strip = thrice_strip // 3
    come = pltpu.make_async_copy(load(0).at[at[2]], piece, arrival.at[0])
    come.start()
    out_ref[:, 2 * strip :] = load(1)[...].reshape(cols, strip, -1)
    store(0, (slice(None), slice(2 * strip, 3 * strip)))
    come.wait()
    out_ref[:, : 2 * strip] = jnp.broadcast_to(piece[...], (cols, *piece.shape))
    store(0, (slice(None), slice(0, 2 * strip)))


def fanned_body(scalars, load, made, store, piece, arrival):
    (at,) = scalars
    strip = piece.shape[0]
    come = pltpu.make_async_copy(load(0).at[at[2], pl.ds(2 * strip, strip)], piece, arrival.at[0])
    come.start()
    come.wait()
    made[0][...] = jnp.broadcast_to(piece[...], made[0].shape)
    store(0)


def taken_off(n, at, load, total, base, b_scr, d_scr):
    a_at, held_at, other_at, right_at, keep_at, got_at = range(base, base + 6)
    core = at[1]
    half, width = d_scr.shape[1:]
    d_scr[core] = load(held_at)[...].reshape(half, width)
    d_scr[1 - core] = load(other_at)[...].reshape(half, width)
    total[...] -= narrow(square_of(load(a_at)), d_scr[...].reshape(width, width))
    b_tile = joined(b_scr, core, load(keep_at), load(got_at))
    row_part = square_of(load(right_at))

    @pl.when(at[3 + n] > 0)
    def _():
        total[...] -= narrow(row_part, b_tile)


def behind_body(scalars, load, made, store, b_scr, d_scr):
    (at,) = scalars
    (total,) = made
    total[...] = load(0)[...]
    for n in range(FRONTS):

        @pl.when(at[7] == n)
        def _(ref=load(1 + n)):
            total[...] = ref[...]

    for k in range(4, 16):
        load(k)

    @pl.when(at[7] == FRONTS)
    def _():
        for n in range(2):
            taken_off(n, at, load, total, 4 + 6 * n, b_scr.at[n], d_scr.at[n])

    store(0)


def behind_last_body(scalars, load, made, store, b_scr, d_scr):
    (at,) = scalars
    (total,) = made
    total[...] = load(0)[...]
    for k in range(1, 7):
        load(k)

    @pl.when(at[7] == FRONTS)
    def _():
        taken_off(2, at, load, total, 1, b_scr, d_scr)

    store(0)


def sweep(work, a_tiles, b_tiles, u_powers, v_powers, shift):
    LOCAL[:] = [work, a_tiles, b_tiles, u_powers, v_powers]
    rows = lax.axis_size("row")
    cols = lax.axis_size("col")
    grid = Grid(rows, cols)
    deep = grid.deep
    i = lax.axis_index("row")
    j = lax.axis_index("col")
    z, core = i // CORES, i % CORES
    diagonal = i + j
    first = max(0, (rows + cols) // 2 - FRONTS)
    last = first + FRONTS - 1
    width = work.shape[0]
    strip = width // cols
    half = width // 2
    tile = (width, width)
    scale = 0.5 / shift

    def place(number):
        kind = jnp.clip(diagonal - first, -1, FRONTS)
        return jnp.stack(
            [z, core, jnp.clip(number - i, 0, cols - 1)]
            + [(i <= first + n).astype(jnp.int32) for n in range(FRONTS)]
            + [(diagonal == number).astype(jnp.int32), kind]
        ).astype(jnp.int32)

    at, at_second, at_last = place(first), place(first + 1), place(last)
    near = {n: set() for n in range(cols)}
    for n in range(FRONTS):
        for r, c in grid.front(first + n):
            near[c].add(r // CORES)
    opening, v_mine, *b_mine = kernel(
        functools.partial(opening_body, (first, rows, cols, deep, strip)),
        [((cols, (2 + FRONTS) * strip, width), half_type), ((2 * strip, width), half_type)]
        + [(((FRONTS + 1) * strip, width), half_type)] * deep,
        (u_powers, (0, slice(0, 1))),
        a_tiles,
        (v_powers, (0, slice(0, 1))),
        b_tiles,
        scalars=(at,),
    )
    opened = exchange(opening, "col")
    v_all = [v_mine] + [
        send(v_mine, grid.deeper(s, lambda k, l: k // CORES in near[l]))
        for s in range(1, deep)
    ]
    b_all = [b_mine[0]] + [
        send(b_mine[s], grid.deeper(s, lambda k, l: k // CORES * CORES + CORES - 1 + l > first))
        for s in range(1, deep)
    ]
    (v_here,) = kernel(
        functools.partial(sorted_v_body, deep), [((deep, 2 * strip, width), half_type)],
        *v_all, scalars=(at,),
    )
    v_there = send(v_here, grid.partner())

    powers = ((3, 2, *tile), half_type)
    u_list, v_list, x_first, s_first = kernel(
        functools.partial(first_body, (deep, strip, width)),
        [powers, powers, (tile, full_type), (tile, half_type)],
        v_here, v_there, (opened, (slice(None), slice(0, 2 * strip))), work,
        scalars=(at, scale), scratch=[pltpu.VMEM((2, rows, strip, width), half_type)],
        when=lambda given: (given[0][7] >= 0) & (given[0][7] < FRONTS),
    )
    hop_down = send(s_first, grid.moved(first, 1, 0))
    hop_right = send(s_first, grid.moved(first, 0, 1))
    far_down = send(s_first, grid.moved(first, 2, 0))
    far_right = send(s_first, grid.moved(first, 0, 2))
    b_keep, b_give = kernel(
        functools.partial(sorted_b_body, deep, strip),
        [((FRONTS, deep, strip, width), half_type)] * 2, *b_all, scalars=(at,),
    )
    b_got = send(b_give, grid.partner())

    def a_of(n):
        return opened, (slice(None), slice((2 + n) * strip, (3 + n) * strip))

    b_scr = pltpu.VMEM((rows, strip, width), half_type)
    b_more = pltpu.VMEM((2, rows, strip, width), half_type)
    d_scr = pltpu.VMEM((2, half, width), half_type)
    more = [(u_list, slice(1, 3)), (v_list, slice(1, 3))]

    halves = ((1, half, width), half_type)
    both = ((2, half, width), half_type)
    x_second, s_second, t_mine, t_give, third_operand = kernel(
        functools.partial(next_body, 1),
        [(tile, full_type), (tile, half_type), both, both, ((cols, 2 * strip, width), half_type)],
        (u_list, 0), (v_list, 0), work, a_of(0), hop_down, hop_right, (b_keep, 0), (b_got, 0), *more,
        scalars=(at_second, scale), scratch=[b_more], late=(8, 9),
        when=lambda given: given[0][6] > 0, other=nothing_sent,
    )
    hop_down = send(s_second, grid.moved(first + 1, 1, 0))
    hop_right = send(s_second, grid.moved(first + 1, 0, 1))
    third = exchange(third_operand, "col")

    x_third, s_third, l_mine, l_give = kernel(
        functools.partial(next_body, 2),
        [(tile, full_type), (tile, half_type), halves, halves],
        (u_list, 0), (v_list, 0), work,
        a_of(0), far_down, far_right, (b_keep, 0), (b_got, 0),
        a_of(1), hop_down, hop_right, (b_keep, 1), (b_got, 1), *more,
        scalars=(at_last, scale), scratch=[b_more], late=(13, 14),
        when=lambda given: given[0][6] > 0, other=nothing_sent,
    )
    one = pltpu.SemaphoreType.DMA((1,))
    (fourth_operand,) = kernel(
        packed_body, [((cols, 3 * strip, width), half_type)], (third, "raw"), s_third,
        scalars=(at_second,), scratch=[pltpu.VMEM((2 * strip, width), half_type), one],
    )
    fourth = exchange(fourth_operand, "col")
    (fifth_operand,) = kernel(
        fanned_body, [((cols, strip, width), half_type)], (fourth, "raw"),
        scalars=(at_last,), scratch=[pltpu.VMEM((strip, width), half_type), one],
    )
    fifth = exchange(fifth_operand, "col")

    def spread_deep(mine, give, number):
        given = send(give, grid.partner())
        held = mine + given
        for pairs in grid.tree(number, last):
            got = send(held, pairs)
            held = held + got
        return held, send(held, grid.partner())

    t_held, t_other = spread_deep(t_mine, t_give, first + 1)
    l_held, l_other = spread_deep(l_mine, l_give, last)

    factors = []
    for n in range(2):
        factors += [
            a_of(n), (t_held, n), (t_other, n),
            (fourth, (slice(None), slice(n * strip, (n + 1) * strip))), (b_keep, n), (b_got, n),
        ]
    (behind,) = kernel(
        behind_body, [(tile, full_type)], work, x_first, x_second, x_third, *factors,
        scalars=(at,), scratch=[b_more, pltpu.VMEM((2, 2, half, width), half_type)],
    )
    (result,) = kernel(
        behind_last_body, [(tile, full_type)],
        behind, a_of(2), l_held, l_other, fifth, (b_keep, 2), (b_got, 2),
        scalars=(at,), scratch=[b_scr, d_scr],
    )
    return result


def solution(mesh):
    placed = (
        P("row", "col"),
        P("row", None, "col", None),
        P(None, "col", "row", None),
        P("row", None, "col", None),
        P("col", None, "row", None),
        P(),
    )
    return jax.shard_map(
        sweep, mesh=mesh, in_specs=placed, out_specs=P("row", "col"), check_vma=False
    )
```
